128 devices in a mesh: user: 16 (over y_lo, x, core), item: 8 (over z, y_hi).
Axes of the slice: x: 4, y: 4 (y_hi: 2, y_lo: 2; y = y_hi * 2 + y_lo), z: 4, core: 2. Of those that a mesh axis runs over, the one named last changes fastest.
Arguments:
- u_factors: float32 [262144, 256], P(('user', 'item')), may hold values from -1.5 to 1.5
- v_factors: float32 [32768, 256], P(('item', 'user')), may hold values from -1.5 to 1.5
- ratings: bfloat16 [16, 8, 2, 224, 128, 128], P('user', 'item'), may hold values from -6 to 6
- tile_rows: int32 [16, 8, 2, 224], P('user', 'item'), may hold values from 0 to 15, as said below
- tile_cols: int32 [16, 8, 2, 224], P('user', 'item'), may hold values from 0 to 31
- tile_counts: int32 [16, 8, 2], P('user', 'item'), may hold values from 28 to 224, as said below
- u_noise: bfloat16 [2, 262144, 256], P(None, ('user', 'item')), may hold values from -6 to 6
- v_noise: bfloat16 [2, 32768, 256], P(None, ('item', 'user')), may hold values from -6 to 6
Outputs:
- new_users: float32 [262144, 256], P(('user', 'item'))
- new_items: float32 [32768, 256], P(('item', 'user'))
The draws below stay inside these ranges and needn't reach their ends.
Inputs may be any that keep to these rules, and one draw needn't show every extreme that they name: Within one list of a block and sub-epoch the (tile_rows, tile_cols) pairs are distinct over all 224 slots. `tile_counts`: some list in every draw is full and some has the smallest count.
All inputs are finite; a program needn't handle non-finite values.
Results may differ from the reference program's by a relative error of at most 0.00115.
Values may be sent and summed in bfloat16 or wider, within the bound.
A program may use at most 128 MiB of HBM per device.

```python
import math
import jax
import jax.numpy as jnp
from jax import lax

K = 256
TILE = 128
UT = 16
IT = 32
TPB = 224
SUBS = 2
USERS = 262144
ITEMS = 32768
N_USER = 16
N_ITEM = 8


def slot_lists(key):
    cells = N_USER * N_ITEM * SUBS
    subkeys = jax.random.split(jax.random.fold_in(key, 17), cells)
    slots = jax.vmap(lambda subkey: jax.random.permutation(subkey, UT * IT)[:TPB])(subkeys)
    return slots.reshape(N_USER, N_ITEM, SUBS, TPB).astype(jnp.int32)


def draw_tile_rows(key, part):
    return slot_lists(key) // IT


def draw_tile_cols(key, part):
    return slot_lists(key) % IT


def draw_tile_counts(key, part):
    cells = N_USER * N_ITEM * SUBS
    lowest = max(1, TPB // 8)
    spread = TPB - lowest
    keys = jax.random.split(jax.random.fold_in(key, 29), 4)
    first = jax.random.randint(keys[0], (cells,), 0, spread + 1)
    second = jax.random.randint(keys[1], (cells,), 0, spread + 1)
    counts = lowest + first * second // max(spread, 1)
    fullest = jax.random.randint(keys[2], (), 0, cells)
    emptiest = (fullest + 1 + jax.random.randint(keys[3], (), 0, cells - 1)) % cells
    places = jnp.arange(cells)
    counts = jnp.where(places == fullest, TPB, counts)
    counts = jnp.where(places == emptiest, lowest, counts)
    return counts.reshape(N_USER, N_ITEM, SUBS).astype(jnp.int32)


def block_levels(own_key, shape, cuts, smallest, high):
    level, own = 1.0, jax.random.fold_in(own_key, 6)
    for position, parts in cuts:
        heights = jnp.exp(jax.random.uniform(jax.random.fold_in(own, position), (parts,), jnp.float32, smallest / len(cuts), high / len(cuts)))
        level = level * jnp.repeat(heights, shape[position] // parts).reshape([-1 if axis == position else 1 for axis in range(len(shape))])
    return level


def scatter_about(rng, shape, scale, reach, shards=(), kind=jnp.bfloat16):
    values = scale * jax.random.normal(rng, shape, jnp.float32)
    if shards:
        values = values * block_levels(rng, shape, shards, -0.22, 0.18)
    return jnp.clip(values, -reach, reach).astype(kind)


def setup_inputs(seed: int = 0) -> dict:
    streams_of = jax.random.split(jax.random.key(seed), 9)
    return {
        "u_factors": scatter_about(streams_of[0], (USERS, K), 0.25, 1.5, ((0, 128),), jnp.float32),
        "v_factors": scatter_about(streams_of[1], (ITEMS, K), 0.25, 1.5, ((0, 128),), jnp.float32),
        "ratings": scatter_about(streams_of[2], (N_USER, N_ITEM, SUBS, TPB, TILE, TILE), 1.0, 6.0, ((0, 16), (1, 8))),
        "tile_rows": draw_tile_rows(jax.random.fold_in(streams_of[8], 71), 0),
        "tile_cols": draw_tile_cols(jax.random.fold_in(streams_of[8], 71), 0),
        "tile_counts": draw_tile_counts(jax.random.fold_in(streams_of[8], 71), 0),
        "u_noise": scatter_about(streams_of[6], (SUBS, USERS, K), 1.0, 6.0, ((1, 128),)),
        "v_noise": scatter_about(streams_of[7], (SUBS, ITEMS, K), 1.0, 6.0, ((1, 128),)),
    }


STEP_SIZE = 0.004
PRIOR = 25.0

def reference(u_factors, v_factors, ratings, tile_rows, tile_cols, tile_counts, u_noise, v_noise):
    power = float(N_ITEM)
    half_step = 0.5 * STEP_SIZE
    root_step = math.sqrt(STEP_SIZE)
    user_rows = UT * TILE
    group_rows = IT * TILE
    users_now = u_factors
    items_now = v_factors
    for section in range(SUBS):
        users_bf = users_now.astype(jnp.bfloat16)
        items_bf = items_now.astype(jnp.bfloat16)

        def block_work(carry, block):
            urow = block // N_ITEM
            icol = block % N_ITEM
            group = (icol - section) % N_ITEM
            user_tiles = lax.dynamic_slice_in_dim(users_bf, (block * user_rows).astype(jnp.int32), user_rows, 0)
            user_tiles = user_tiles.reshape(UT, TILE, K).astype(jnp.float32)
            item_tiles = lax.dynamic_slice_in_dim(items_bf, (group * group_rows).astype(jnp.int32), group_rows, 0)
            item_tiles = item_tiles.reshape(IT, TILE, K).astype(jnp.float32)
            rating_list = ratings[urow, icol, section]
            row_list = tile_rows[urow, icol, section]
            col_list = tile_cols[urow, icol, section]
            live_count = tile_counts[urow, icol, section]
            user_part = user_tiles[row_list]
            item_part = item_tiles[col_list]
            predicted = jnp.einsum('tak,tbk->tab', user_part, item_part)
            live = jnp.arange(TPB) < live_count
            misfit = jnp.where(live[:, None, None], rating_list.astype(jnp.float32) - predicted, 0.0).astype(jnp.bfloat16)
            misfit = lax.optimization_barrier(misfit).astype(jnp.float32)
            grad_user = jnp.zeros((UT, TILE, K), jnp.float32).at[row_list].add(jnp.einsum('tab,tbk->tak', misfit, item_part))
            grad_group = jnp.zeros((IT, TILE, K), jnp.float32).at[col_list].add(jnp.einsum('tab,tak->tbk', misfit, user_part))
            carry = carry.at[group].add(grad_group)
            return (carry, grad_user.reshape(user_rows, K))
        grad_items, grad_users = lax.scan(block_work, jnp.zeros((N_ITEM, IT, TILE, K), jnp.float32), jnp.arange(N_USER * N_ITEM, dtype=jnp.int32))
        grad_users = grad_users.reshape(USERS, K)
        grad_items = grad_items.reshape(ITEMS, K)
        users_now = users_now + half_step * (power * grad_users - PRIOR * users_now) + root_step * u_noise[section].astype(jnp.float32)
        noise_items = jnp.roll(v_noise[section].astype(jnp.float32).reshape(N_ITEM, group_rows, K), -section, axis=0).reshape(ITEMS, K)
        items_now = items_now + half_step * (power * grad_items - PRIOR * items_now) + root_step * noise_items
    return (users_now, items_now)
```

```python
import functools
import math

import jax
import jax.numpy as jnp
from jax import lax
from jax.experimental import pallas as pl
from jax.experimental.pallas import tpu as pltpu
from jax.sharding import PartitionSpec as P

HALF_STEP = 0.002
ROOT_STEP = math.sqrt(0.004)
PRIOR = 25.0
GROUP = 8


def shifted(x, axis, by):
    peers = lax.axis_size(axis)
    return lax.ppermute(x, axis, [(i, (i + by) % peers) for i in range(peers)])


def tile_kernel(section, rows, cols, count, user_ref, item_ref, rating_ref, gu_ref, gv_ref, misfit_ref):
    gu_ref[...] = jnp.zeros_like(gu_ref)
    gv_ref[...] = jnp.zeros_like(gv_ref)
    live = count[section]

    def predict(step, slot):
        for q in range(GROUP):
            t = step * GROUP + q
            predicted = lax.dot_general(
                user_ref[rows[section, t]],
                item_ref[cols[section, t]],
                (((1,), (1,)), ((), ())),
                preferred_element_type=jnp.float32,
            )
            misfit = jnp.where(t < live, rating_ref[0, t].astype(jnp.float32) - predicted, 0.0)
            misfit_ref[slot * GROUP + q] = misfit.astype(jnp.bfloat16)

    def grads(step, slot):
        parts = []
        for q in range(GROUP):
            t = step * GROUP + q
            misfit = misfit_ref[slot * GROUP + q]
            parts.append(
                (
                    jnp.dot(misfit, item_ref[cols[section, t]], preferred_element_type=jnp.float32),
                    lax.dot_general(
                        misfit,
                        user_ref[rows[section, t]],
                        (((0,), (0,)), ((), ())),
                        preferred_element_type=jnp.float32,
                    ),
                )
            )
        for q in range(GROUP):
            t = step * GROUP + q
            gu_ref[rows[section, t]] += parts[q][0]
            gv_ref[cols[section, t]] += parts[q][1]

    steps = (live + GROUP - 1) // GROUP
    predict(0, 0)

    def advance(step, _):
        slot = lax.rem(step, 2)
        grads(step, slot)
        predict(jnp.minimum(step + 1, steps - 1), 1 - slot)
        return 0

    lax.fori_loop(0, steps, advance, 0)


def tile_grads(section, user_bf, group_bf, ratings, rows, cols, counts):
    tile = ratings.shape[-1]
    listed = ratings.shape[1]
    width = user_bf.shape[1]
    user_tiles = user_bf.reshape(-1, tile, width)
    item_tiles = group_bf.reshape(-1, tile, width)
    grad_user, grad_item = pl.pallas_call(
        functools.partial(tile_kernel, section),
        grid=(1,),
        out_shape=(
            jax.ShapeDtypeStruct(user_tiles.shape, jnp.float32),
            jax.ShapeDtypeStruct(item_tiles.shape, jnp.float32),
        ),
        in_specs=[
            pl.BlockSpec(memory_space=pltpu.SMEM),
            pl.BlockSpec(memory_space=pltpu.SMEM),
            pl.BlockSpec(memory_space=pltpu.SMEM),
            pl.BlockSpec(user_tiles.shape, lambda i: (0, 0, 0), pipeline_mode=pl.Buffered(1)),
            pl.BlockSpec(item_tiles.shape, lambda i: (0, 0, 0), pipeline_mode=pl.Buffered(1)),
            pl.BlockSpec((1, listed, tile, tile), lambda i: (section, 0, 0, 0), pipeline_mode=pl.Buffered(1)),
        ],
        out_specs=(
            pl.BlockSpec(user_tiles.shape, lambda i: (0, 0, 0)),
            pl.BlockSpec(item_tiles.shape, lambda i: (0, 0, 0)),
        ),
        scratch_shapes=[pltpu.VMEM((2 * GROUP, tile, tile), jnp.bfloat16)],
        compiler_params=pltpu.CompilerParams(vmem_limit_bytes=48 * 1024 * 1024),
    )(rows, cols, counts, user_tiles, item_tiles, ratings)
    return grad_user.reshape(user_bf.shape), grad_item.reshape(group_bf.shape)


def body(u_factors, v_factors, ratings, tile_rows, tile_cols, tile_counts, u_noise, v_noise):
    sections = ratings.shape[2]
    power = float(lax.axis_size("item"))
    user_master = u_factors
    item_master = v_factors
    for section in range(sections):
        group_bf = lax.all_gather(item_master.astype(jnp.bfloat16), "user", axis=0, tiled=True)
        grad_user, grad_item = tile_grads(
            section,
            user_master.astype(jnp.bfloat16),
            group_bf,
            ratings[0, 0],
            tile_rows[0, 0],
            tile_cols[0, 0],
            tile_counts[0, 0],
        )
        user_master = (
            user_master
            + HALF_STEP * (power * grad_user - PRIOR * user_master)
            + ROOT_STEP * u_noise[section].astype(jnp.float32)
        )
        owned = lax.psum_scatter(grad_item, "user", scatter_dimension=0, tiled=True)
        item_master = (
            item_master
            + HALF_STEP * (power * owned - PRIOR * item_master)
            + ROOT_STEP * v_noise[section].astype(jnp.float32)
        )
        if section + 1 < sections:
            item_master = shifted(item_master, "item", 1)
    item_master = shifted(item_master, "item", 1 - sections)
    return (user_master, item_master)


def solution(mesh):
    placed = (
        P(("user", "item"), None),
        P(("item", "user"), None),
        P("user", "item", None, None, None, None),
        P("user", "item", None, None),
        P("user", "item", None, None),
        P("user", "item", None),
        P(None, ("user", "item"), None),
        P(None, ("item", "user"), None),
    )
    return jax.shard_map(
        body,
        mesh=mesh,
        in_specs=placed,
        out_specs=(P(("user", "item"), None), P(("item", "user"), None)),
        check_vma=False,
    )
```

```python
import math

import jax
import jax.numpy as jnp
from jax import lax
from jax.experimental import pallas as pl
from jax.experimental.pallas import tpu as pltpu
from jax.sharding import PartitionSpec as P

HALF_STEP = 0.002
ROOT_STEP = math.sqrt(0.004)
PRIOR = 25.0
LEVELS = 32767.0
MESH = pl.DeviceIdType.MESH

TILE = 128
WIDTH = 256
BLOCK = 2048
OWNED = 256
CHIPS = 8
ITEM_PEERS = 8
BAND = 256
BANDS = BLOCK // BAND


def visit(o, chip):
    turn = lax.rem(o, 3)
    dx = jnp.where(o < 6, turn + turn // 2, 2)
    dy = jnp.where(o < 6, o // 3, o - 6)
    return lax.rem(chip // 4 + dy, 2) * 4 + lax.rem(lax.rem(chip, 4) + dx, 4)


def whole_kernel(
    power,
    slots,
    u_hbm,
    v_hbm,
    rating_hbm,
    un_hbm,
    vn_hbm,
    uout_hbm,
    vout_hbm,
    ratings_0,
    ratings_1,
    u_now,
    u_bf,
    u_turned,
    grad_u,
    u_noise,
    v_now,
    v_noise,
    v_next,
    v_bf,
    group,
    misfit,
    grad_v,
    from_twin,
    packed,
    scales,
    packed_in,
    scales_in,
    total,
    load_sem,
    ag_send,
    ag_recv,
    twin_send,
    twin_recv,
    q_send,
    q_recv,
    s_send,
    s_recv,
    hop_send,
    hop_recv,
):
    user = lax.axis_index("user")
    item = lax.axis_index("item")
    chip = user // 2
    core = lax.rem(user, 2)
    twin = (chip * 2 + 1 - core, item)
    onward = (user, lax.rem(item + 1, ITEM_PEERS))
    back = (user, lax.rem(item + ITEM_PEERS - 1, ITEM_PEERS))

    def there(o):
        return (visit(o, chip) * 2 + core, item)

    ratings = (ratings_0, ratings_1)
    loads = [
        pltpu.make_async_copy(v_hbm, v_now, load_sem.at[0]),
        pltpu.make_async_copy(u_hbm, u_now, load_sem.at[1]),
        pltpu.make_async_copy(rating_hbm.at[0], ratings_0, load_sem.at[2]),
        pltpu.make_async_copy(un_hbm, u_noise, load_sem.at[3]),
        pltpu.make_async_copy(vn_hbm, v_noise, load_sem.at[4]),
        pltpu.make_async_copy(rating_hbm.at[1], ratings_1, load_sem.at[5]),
    ]
    for load in loads:
        load.start()

    barrier = pltpu.get_barrier_semaphore()
    for peer in [twin, onward, back]:
        pl.semaphore_signal(barrier, inc=1, device_id=peer, device_id_type=MESH)

    def greet(o, _):
        pl.semaphore_signal(barrier, inc=1, device_id=there(o), device_id_type=MESH)
        return 0

    lax.fori_loop(1, CHIPS, greet, 0)
    loads[0].wait()
    group[0, user] = v_now[...].astype(jnp.bfloat16)
    pl.semaphore_wait(barrier, 3 + CHIPS - 1)

    def remote(src, dst, send, recv, device):
        return pltpu.make_async_remote_copy(
            src_ref=src, dst_ref=dst, send_sem=send, recv_sem=recv, device_id=device, device_id_type=MESH
        )

    def ag_copy(s, owner, lane, device):
        at = group.at[s, owner]
        return remote(at, at, ag_send.at[s, lane], ag_recv.at[s, owner], device)

    def spread(s):
        ag_copy(s, user, 0, twin).start()

        def one(o, _):
            ag_copy(s, user, o, there(o)).start()
            return 0

        lax.fori_loop(1, CHIPS, one, 0)

    def twin_copy(s, o):
        return remote(
            grad_v.at[o, 1 - core], from_twin.at[s, o], twin_send.at[s, o], twin_recv.at[s, o], twin
        )

    def q_copy(s, o, slot):
        return remote(packed.at[o], packed_in.at[s, slot], q_send.at[s, o], q_recv.at[s, slot], there(o))

    def s_copy(s, o, slot):
        return remote(scales.at[o], scales_in.at[s, slot], s_send.at[s, o], s_recv.at[s, slot], there(o))

    def prepare(s):
        def one(b, _):
            rows = pl.ds(pl.multiple_of(b * BAND, BAND), BAND)
            now = u_now[rows, :]
            if s > 0:
                now = (
                    now
                    + HALF_STEP * (power * grad_u[rows, :] - PRIOR * now)
                    + ROOT_STEP * u_noise[s - 1, rows, :].astype(jnp.float32)
                )
                u_now[rows, :] = now
            if s < 2:
                u_bf[rows, :] = now.astype(jnp.bfloat16)
                u_turned[:, rows] = now.T.astype(jnp.bfloat16)
                grad_u[rows, :] = jnp.zeros((BAND, WIDTH), jnp.float32)
            return 0

        lax.fori_loop(0, BANDS, one, 0)

    def work(s, o, chip_now, half):
        owner = chip_now * 2 + half
        items = group[s, owner]
        for b in range(BANDS):
            rows = pl.ds(b * BAND, BAND)
            predicted = lax.dot_general(
                u_bf[rows, :], items, (((1,), (1,)), ((), ())), preferred_element_type=jnp.float32
            )
            for i in range(BAND // TILE):
                for j in range(OWNED // TILE):
                    at = slots[s, (b * (BAND // TILE) + i) * 32 + owner * 2 + j]
                    rating = ratings[s][jnp.maximum(at, 0)].astype(jnp.float32)
                    part = predicted[i * TILE : (i + 1) * TILE, j * TILE : (j + 1) * TILE]
                    misfit[pl.ds(b * BAND + i * TILE, TILE), pl.ds(j * TILE, TILE)] = jnp.where(
                        at >= 0, rating - part, 0.0
                    ).astype(jnp.bfloat16)
            grad_u[rows, :] += jnp.dot(misfit[rows, :], items, preferred_element_type=jnp.float32)
        grad_v[o, half] = jnp.dot(u_turned[...], misfit[...], preferred_element_type=jnp.float32)

    def finish(s, o):
        twin_copy(s, o).wait_recv()
        term = grad_v[o, core] + from_twin[s, o]
        peak = jnp.max(jnp.abs(term), axis=0, keepdims=True)
        inverse = jnp.where(peak > 1e-30, LEVELS / jnp.maximum(peak, 1e-30), 0.0)
        packed[o] = jnp.round(term * inverse).astype(jnp.int32).astype(jnp.int16)
        scales[o] = jnp.broadcast_to(peak * (1.0 / LEVELS), (8, OWNED))
        q_copy(s, o, chip).start()
        s_copy(s, o, chip).start()

    def section(s):
        def meet(o, _):
            chip_now = visit(o, chip)
            work(s, o, chip_now, core)

            @pl.when(o + 1 < CHIPS)
            def _():
                owner = visit(o + 1, chip) * 2 + core
                ag_copy(s, owner, 0, twin).wait_recv()
                ag_copy(s, owner, CHIPS + o + 1, twin).start()

            ag_copy(s, chip_now * 2 + 1 - core, 0, twin).wait_recv()
            work(s, o, chip_now, 1 - core)
            twin_copy(s, o).start()

            @pl.when(o > 1)
            def _():
                finish(s, o - 1)

            return 0

        lax.fori_loop(0, CHIPS, meet, 0)
        finish(s, CHIPS - 1)

    def own_sum(s):
        twin_copy(s, 0).wait_recv()
        total[...] = grad_v[0, core] + from_twin[s, 0]

        def add(o, _):
            slot = visit(o, chip)
            q_copy(s, o, slot).wait_recv()
            s_copy(s, o, slot).wait_recv()
            total[...] += packed_in[s, slot].astype(jnp.int32).astype(jnp.float32) * scales_in[s, slot, 0:1, :]
            return 0

        lax.fori_loop(1, CHIPS, add, 0)
        return total[...].T

    def settle(s):
        ag_copy(s, user, 0, twin).wait_send()
        twin_copy(s, 0).wait_send()

        def one(o, _):
            ag_copy(s, user, o, there(o)).wait_send()
            ag_copy(s, user, CHIPS + o, twin).wait_send()
            twin_copy(s, o).wait_send()
            q_copy(s, o, chip).wait_send()
            s_copy(s, o, chip).wait_send()
            return 0

        lax.fori_loop(1, CHIPS, one, 0)

    spread(0)
    loads[1].wait()
    prepare(0)
    loads[2].wait()
    section(0)
    loads[3].wait()
    prepare(1)
    loads[4].wait()
    now = v_now[...]
    now = now + HALF_STEP * (power * own_sum(0) - PRIOR * now) + ROOT_STEP * v_noise[0].astype(jnp.float32)
    v_bf[...] = now.astype(jnp.bfloat16)
    hop = remote(v_bf, group.at[1, user], hop_send.at[0], hop_recv.at[0], onward)
    hop.start()
    v_now[...] = now
    hop_full = remote(v_now, v_next, hop_send.at[1], hop_recv.at[1], onward)
    hop_full.start()
    settle(0)
    hop.wait_recv()

    spread(1)
    loads[5].wait()
    section(1)
    prepare(2)
    store = pltpu.make_async_copy(u_now, uout_hbm, load_sem.at[6])
    store.start()
    hop_full.wait()
    now = v_next[...]
    v_next[...] = (
        now + HALF_STEP * (power * own_sum(1) - PRIOR * now) + ROOT_STEP * v_noise[1].astype(jnp.float32)
    )
    home = remote(v_next, vout_hbm, hop_send.at[2], hop_recv.at[2], back)
    home.start()
    settle(1)
    hop.wait_send()
    store.wait()
    home.wait()


def slot_map(rows, cols, counts):
    sections, listed = rows.shape
    cell = jnp.arange(512, dtype=jnp.int32)[None, :, None]
    slot = jnp.arange(listed, dtype=jnp.int32)
    hit = (rows * 32 + cols)[:, None, :] == cell
    live = (slot[None, :] < counts[:, None])[:, None, :]
    return jnp.max(jnp.where(hit & live, slot[None, None, :], -1), axis=2)


def body(u_factors, v_factors, ratings, tile_rows, tile_cols, tile_counts, u_noise, v_noise):
    slots = slot_map(tile_rows[0, 0], tile_cols[0, 0], tile_counts[0, 0])
    listed = ratings.shape[3]
    power = float(lax.axis_size("item"))
    anywhere = pl.BlockSpec(memory_space=pl.ANY)
    dma = pltpu.SemaphoreType.DMA

    def kernel(*refs):
        whole_kernel(power, *refs)

    return pl.pallas_call(
        kernel,
        out_shape=(
            jax.ShapeDtypeStruct(u_factors.shape, jnp.float32),
            jax.ShapeDtypeStruct(v_factors.shape, jnp.float32),
        ),
        in_specs=[pl.BlockSpec(memory_space=pltpu.SMEM)] + [anywhere] * 5,
        out_specs=(anywhere, anywhere),
        scratch_shapes=[
            pltpu.VMEM((listed, TILE, TILE), jnp.bfloat16),
            pltpu.VMEM((listed, TILE, TILE), jnp.bfloat16),
            pltpu.VMEM((BLOCK, WIDTH), jnp.float32),
            pltpu.VMEM((BLOCK, WIDTH), jnp.bfloat16),
            pltpu.VMEM((WIDTH, BLOCK), jnp.bfloat16),
            pltpu.VMEM((BLOCK, WIDTH), jnp.float32),
            pltpu.VMEM((2, BLOCK, WIDTH), jnp.bfloat16),
            pltpu.VMEM((OWNED, WIDTH), jnp.float32),
            pltpu.VMEM((2, OWNED, WIDTH), jnp.bfloat16),
            pltpu.VMEM((OWNED, WIDTH), jnp.float32),
            pltpu.VMEM((OWNED, WIDTH), jnp.bfloat16),
            pltpu.VMEM((2, 2 * CHIPS, OWNED, WIDTH), jnp.bfloat16),
            pltpu.VMEM((BLOCK, OWNED), jnp.bfloat16),
            pltpu.VMEM((CHIPS, 2, WIDTH, OWNED), jnp.float32),
            pltpu.VMEM((2, CHIPS, WIDTH, OWNED), jnp.float32),
            pltpu.VMEM((CHIPS, WIDTH, OWNED), jnp.int16),
            pltpu.VMEM((CHIPS, 8, OWNED), jnp.float32),
            pltpu.VMEM((2, CHIPS, WIDTH, OWNED), jnp.int16),
            pltpu.VMEM((2, CHIPS, 8, OWNED), jnp.float32),
            pltpu.VMEM((WIDTH, OWNED), jnp.float32),
            dma((7,)),
            dma((2, 2 * CHIPS)),
            dma((2, 2 * CHIPS)),
            dma((2, CHIPS)),
            dma((2, CHIPS)),
            dma((2, CHIPS)),
            dma((2, CHIPS)),
            dma((2, CHIPS)),
            dma((2, CHIPS)),
            dma((3,)),
            dma((3,)),
        ],
        compiler_params=pltpu.CompilerParams(
            collective_id=0, has_side_effects=True, vmem_limit_bytes=60 * 1024 * 1024
        ),
    )(slots, u_factors, v_factors, ratings[0, 0], u_noise, v_noise)


def solution(mesh):
    placed = (
        P(("user", "item"), None),
        P(("item", "user"), None),
        P("user", "item", None, None, None, None),
        P("user", "item", None, None),
        P("user", "item", None, None),
        P("user", "item", None),
        P(None, ("user", "item"), None),
        P(None, ("item", "user"), None),
    )
    return jax.shard_map(
        body,
        mesh=mesh,
        in_specs=placed,
        out_specs=(P(("user", "item"), None), P(("item", "user"), None)),
        check_vma=False,
    )
```

```python
import math

import jax
import jax.numpy as jnp
from jax import lax
from jax.experimental import pallas as pl
from jax.experimental.pallas import tpu as pltpu
from jax.sharding import PartitionSpec as P

HALF_STEP = 0.002
ROOT_STEP = math.sqrt(0.004)
PRIOR = 25.0
LEVELS = 32767.0
MESH = pl.DeviceIdType.MESH

TILE = 128
WIDTH = 256
BLOCK = 2048
OWNED = 256
CHIPS = 8
ITEM_PEERS = 8
BAND = 256
BANDS = BLOCK // BAND


VISIT_Y = (0, 0, 1, 0, 1, 1, 1, 0)
VISIT_X = (0, 3, 0, 2, 3, 2, 1, 1)
SWAP = 6


def pick(o, table):
    total = 0
    for k, value in enumerate(table):
        if value:
            total = total + jnp.where(o == k, value, 0)
    return total


def offset(chip, dy, dx):
    return lax.rem(chip // 4 + dy, 2) * 4 + lax.rem(lax.rem(chip, 4) + 4 + dx, 4)


def visit(o, chip):
    return offset(chip, pick(o, VISIT_Y), pick(o, VISIT_X))


def visitor(o, chip):
    return offset(chip, pick(o, VISIT_Y), -pick(o, VISIT_X))


def whole_kernel(
    power,
    slots,
    u_hbm,
    v_hbm,
    rating_hbm,
    un_hbm,
    vn_hbm,
    uout_hbm,
    vout_hbm,
    ratings_0,
    ratings_1,
    u_now,
    u_bf,
    u_turned,
    grad_u,
    u_noise,
    v_now,
    v_noise,
    noise_home,
    v_bf,
    group,
    misfit_a,
    misfit_b,
    grad_v,
    from_twin,
    packed,
    scales,
    packed_in,
    scales_in,
    total,
    load_sem,
    ag_send,
    ag_recv,
    twin_send,
    twin_recv,
    q_send,
    q_recv,
    s_send,
    s_recv,
    hop_send,
    hop_recv,
):
    user = lax.axis_index("user")
    item = lax.axis_index("item")
    chip = user // 2
    core = lax.rem(user, 2)
    twin = (chip * 2 + 1 - core, item)
    across = offset(chip, 1, 0) * 2 + core
    next_item = lax.rem(item + 1, ITEM_PEERS)
    last_item = lax.rem(item + ITEM_PEERS - 1, ITEM_PEERS)
    onward = (across, next_item)
    back = (across, last_item)

    def seen(o):
        return (visit(o, chip) * 2 + core, item)

    def at(dy, dx):
        return (offset(chip, dy, dx) * 2 + core, item)

    ratings = (ratings_0, ratings_1)
    load_v = pltpu.make_async_copy(v_hbm, v_now, load_sem.at[0])
    load_u = pltpu.make_async_copy(u_hbm, u_now, load_sem.at[1])
    load_0 = pltpu.make_async_copy(rating_hbm.at[0], ratings_0, load_sem.at[2])
    load_un = pltpu.make_async_copy(un_hbm, u_noise, load_sem.at[3])
    load_vn = pltpu.make_async_copy(vn_hbm, v_noise, load_sem.at[4])
    load_1 = pltpu.make_async_copy(rating_hbm.at[1], ratings_1, load_sem.at[5])
    barrier = pltpu.get_barrier_semaphore()
    for peer in [onward, back, (user, next_item), (user, last_item), twin]:
        pl.semaphore_signal(barrier, inc=1, device_id=peer, device_id_type=MESH)

    def greet(o, _):
        pl.semaphore_signal(barrier, inc=1, device_id=seen(CHIPS - o), device_id_type=MESH)
        return 0

    lax.fori_loop(1, CHIPS, greet, 0)
    load_v.start()
    load_u.start()
    load_0.start()
    load_vn.start()

    def remote(src, dst, send, recv, device):
        return pltpu.make_async_remote_copy(
            src_ref=src, dst_ref=dst, send_sem=send, recv_sem=recv, device_id=device, device_id_type=MESH
        )

    noise_copy = remote(v_noise.at[1], noise_home, hop_send.at[1], hop_recv.at[1], (user, last_item))

    def ag_copy(s, owner, lane, device):
        at = group.at[s, owner]
        return remote(at, at, ag_send.at[s, lane], ag_recv.at[s, owner], device)

    def spread(s):
        ag_copy(s, user, 1, at(0, 1)).start()
        ag_copy(s, user, 2, at(0, -1)).start()
        ag_copy(s, user, 3, at(1, 0)).start()
        ag_copy(s, user, 0, twin).start()

    def pass_on(s, order, dy, dx):
        owner = offset(chip, dy, dx) * 2 + core
        ag_copy(s, owner, 0, twin).wait_recv()
        ag_copy(s, owner, CHIPS + order, twin).start()
        if (dy, dx) == (1, 0):
            ag_copy(s, owner, 5, at(0, 1)).start()
            ag_copy(s, owner, 6, at(0, -1)).start()
        if (dy, dx) == (0, 2):
            ag_copy(s, owner, 7, at(1, 0)).start()
        if (dy, dx) == (0, -1):

            @pl.when(core == 0)
            def _():
                ag_copy(s, owner, 4, at(0, 1)).start()

        if (dy, dx) == (0, 1):

            @pl.when(core == 1)
            def _():
                ag_copy(s, owner, 4, at(0, -1)).start()

    def twin_copy(s, o):
        return remote(
            grad_v.at[o, 1 - core], from_twin.at[s, o], twin_send.at[s, o], twin_recv.at[s, o], twin
        )

    def q_copy(s, o, slot):
        return remote(packed.at[o], packed_in.at[s, slot], q_send.at[s, o], q_recv.at[s, slot], seen(o))

    def s_copy(s, o, slot):
        return remote(scales.at[o], scales_in.at[s, slot], s_send.at[s, o], s_recv.at[s, slot], seen(o))

    def prepare(s):
        def one(b, _):
            rows = pl.ds(pl.multiple_of(b * BAND, BAND), BAND)
            now = u_now[rows, :]
            if s > 0:
                now = (
                    now
                    + HALF_STEP * (power * grad_u[rows, :] - PRIOR * now)
                    + ROOT_STEP * u_noise[s - 1, rows, :].astype(jnp.float32)
                )
                u_now[rows, :] = now
            if s < 2:
                u_bf[rows, :] = now.astype(jnp.bfloat16)
                u_turned[:, rows] = now.T.astype(jnp.bfloat16)
                grad_u[rows, :] = jnp.zeros((BAND, WIDTH), jnp.float32)
            return 0

        lax.fori_loop(0, BANDS, one, 0)

    def predict(s, owner, misfit):
        items = group[s, owner]
        tiles = 2 * (owner if s == 0 else lax.rem(owner + 8, 16))
        for b in range(BANDS):
            rows = pl.ds(b * BAND, BAND)
            predicted = lax.dot_general(
                u_bf[rows, :], items, (((1,), (1,)), ((), ())), preferred_element_type=jnp.float32
            )
            for i in range(BAND // TILE):
                for j in range(OWNED // TILE):
                    at = slots[s, (b * (BAND // TILE) + i) * 32 + tiles + j]
                    rating = ratings[s][jnp.maximum(at, 0)].astype(jnp.float32)
                    part = predicted[i * TILE : (i + 1) * TILE, j * TILE : (j + 1) * TILE]
                    misfit[pl.ds(b * BAND + i * TILE, TILE), pl.ds(j * TILE, TILE)] = jnp.where(
                        at >= 0, rating - part, 0.0
                    ).astype(jnp.bfloat16)

    def grads(s, o, owner, half, misfit):
        items = group[s, owner]
        for b in range(BANDS):
            rows = pl.ds(b * BAND, BAND)
            grad_u[rows, :] += jnp.dot(misfit[rows, :], items, preferred_element_type=jnp.float32)
        grad_v[o, half] = jnp.dot(u_turned[...], misfit[...], preferred_element_type=jnp.float32)

    def coded(term):
        peak = jnp.max(jnp.abs(term), axis=0, keepdims=True)
        inverse = jnp.where(peak > 1e-30, LEVELS / jnp.maximum(peak, 1e-30), 0.0)
        code = jnp.round(term * inverse).astype(jnp.int32).astype(jnp.int16)
        return code, jnp.broadcast_to(peak * (1.0 / LEVELS), (8, OWNED))

    def decoded(code, step):
        return code.astype(jnp.int32).astype(jnp.float32) * step[0:1, :]

    def finish(s, o):
        twin_copy(s, o).wait_recv()
        packed[o], scales[o] = coded(grad_v[o, core] + from_twin[s, o])
        q_copy(s, o, chip).start()
        s_copy(s, o, chip).start()

    def half_of(o, second):
        first = jnp.where(o < SWAP, core, 1 - core)
        return 1 - first if second else first

    def owner_of(o, second):
        return visit(o, chip) * 2 + half_of(o, second)

    def await_twin(s, o):
        ag_copy(s, visit(o, chip) * 2 + 1 - core, 0, twin).wait_recv()

    def first_block(s, o):
        @pl.when(o < SWAP)
        def _():
            await_twin(s, o)

        predict(s, owner_of(o, True), misfit_b)
        grads(s, o, owner_of(o, False), half_of(o, False), misfit_a)

        @pl.when(o >= SWAP)
        def _():
            twin_copy(s, o).start()

        @pl.when(o > 1)
        def _():
            finish(s, o - 1)

    def section(s):
        predict(s, user, misfit_a)

        def meet(o, _):
            first_block(s, o)

            @pl.when(o == 0)
            def _():
                pass_on(s, 1, 0, -1)

            @pl.when(o == 2)
            def _():
                pass_on(s, 6, 0, 2)

            @pl.when(o == 4)
            def _():
                pass_on(s, 7, 1, 2)

            @pl.when(o + 1 >= SWAP)
            def _():
                await_twin(s, o + 1)

            predict(s, owner_of(o + 1, False), misfit_a)
            grads(s, o, owner_of(o, True), half_of(o, True), misfit_b)

            @pl.when(o < SWAP)
            def _():
                twin_copy(s, o).start()

            @pl.when(o == 0)
            def _():
                pass_on(s, 2, 1, 0)
                pass_on(s, 3, 0, 1)

            @pl.when(o == 2)
            def _():
                pass_on(s, 4, 1, -1)
                pass_on(s, 5, 1, 1)

            if s == 0:

                @pl.when(o == 1)
                def _():
                    load_1.start()
                    load_un.start()

                @pl.when(o == 5)
                def _():
                    noise_copy.start()

            return 0

        lax.fori_loop(0, CHIPS - 1, meet, 0)
        last = CHIPS - 1
        first_block(s, last)
        grads(s, last, owner_of(last, True), half_of(last, True), misfit_b)
        finish(s, last)

    def own_sum(s):
        twin_copy(s, 0).wait_recv()
        total[...] = grad_v[0, core] + from_twin[s, 0]

        def add(o, _):
            slot = visitor(o, chip)
            q_copy(s, o, slot).wait_recv()
            s_copy(s, o, slot).wait_recv()
            total[...] += decoded(packed_in[s, slot], scales_in[s, slot])
            return 0

        lax.fori_loop(1, CHIPS, add, 0)

    def settle(s):
        ag_copy(s, user, 0, twin).wait_send()
        twin_copy(s, 0).wait_send()

        def one(o, _):
            ag_copy(s, user, o, twin).wait_send()
            ag_copy(s, user, CHIPS + o, twin).wait_send()
            twin_copy(s, o).wait_send()
            q_copy(s, o, chip).wait_send()
            s_copy(s, o, chip).wait_send()
            return 0

        lax.fori_loop(1, CHIPS, one, 0)

    load_u.wait()
    prepare(0)
    load_v.wait()
    group[0, user] = v_now[...].astype(jnp.bfloat16)
    load_vn.wait()
    load_0.wait()
    pl.semaphore_wait(barrier, 5 + CHIPS - 1)
    spread(0)
    section(0)
    load_un.wait()
    prepare(1)
    own_sum(0)
    now = v_now[...]
    now = now + HALF_STEP * (power * total[...].T - PRIOR * now) + ROOT_STEP * v_noise[0].astype(jnp.float32)
    v_bf[...] = now.astype(jnp.bfloat16)
    hop = remote(v_bf, group.at[1, across], hop_send.at[0], hop_recv.at[0], onward)
    hop.start()
    v_now[...] = now
    settle(0)
    hop.wait_recv()

    spread(1)
    load_1.wait()
    section(1)
    prepare(2)
    store_u = pltpu.make_async_copy(u_now, uout_hbm, load_sem.at[1])
    store_u.start()
    own_sum(1)
    packed[0], scales[0] = coded(total[...])
    home = offset(chip, 1, 0)
    home_q = remote(packed.at[0], packed_in.at[1, home], hop_send.at[2], hop_recv.at[2], back)
    home_s = remote(scales.at[0], scales_in.at[1, home], hop_send.at[3], hop_recv.at[3], back)
    home_q.start()
    home_s.start()
    settle(1)
    hop.wait_send()
    noise_copy.wait()
    now = v_now[...]
    now = now - HALF_STEP * PRIOR * now + ROOT_STEP * noise_home[...].astype(jnp.float32)
    home_q.wait()
    home_s.wait()
    v_now[...] = now + HALF_STEP * power * decoded(packed_in[1, chip], scales_in[1, chip]).T
    store_v = pltpu.make_async_copy(v_now, vout_hbm, load_sem.at[0])
    store_v.start()
    store_u.wait()
    store_v.wait()


def slot_map(rows, cols, counts):
    sections, listed = rows.shape
    cell = jnp.arange(512, dtype=jnp.int32)[None, :, None]
    slot = jnp.arange(listed, dtype=jnp.int32)
    hit = (rows * 32 + cols)[:, None, :] == cell
    live = (slot[None, :] < counts[:, None])[:, None, :]
    return jnp.max(jnp.where(hit & live, slot[None, None, :], -1), axis=2)


def body(u_factors, v_factors, ratings, tile_rows, tile_cols, tile_counts, u_noise, v_noise):
    slots = slot_map(tile_rows[0, 0], tile_cols[0, 0], tile_counts[0, 0])
    listed = ratings.shape[3]
    power = float(lax.axis_size("item"))
    anywhere = pl.BlockSpec(memory_space=pl.ANY)
    dma = pltpu.SemaphoreType.DMA

    def kernel(*refs):
        whole_kernel(power, *refs)

    return pl.pallas_call(
        kernel,
        out_shape=(
            jax.ShapeDtypeStruct(u_factors.shape, jnp.float32),
            jax.ShapeDtypeStruct(v_factors.shape, jnp.float32),
        ),
        in_specs=[pl.BlockSpec(memory_space=pltpu.SMEM)] + [anywhere] * 5,
        out_specs=(anywhere, anywhere),
        scratch_shapes=[
            pltpu.VMEM((listed, TILE, TILE), jnp.bfloat16),
            pltpu.VMEM((listed, TILE, TILE), jnp.bfloat16),
            pltpu.VMEM((BLOCK, WIDTH), jnp.float32),
            pltpu.VMEM((BLOCK, WIDTH), jnp.bfloat16),
            pltpu.VMEM((WIDTH, BLOCK), jnp.bfloat16),
            pltpu.VMEM((BLOCK, WIDTH), jnp.float32),
            pltpu.VMEM((2, BLOCK, WIDTH), jnp.bfloat16),
            pltpu.VMEM((OWNED, WIDTH), jnp.float32),
            pltpu.VMEM((2, OWNED, WIDTH), jnp.bfloat16),
            pltpu.VMEM((OWNED, WIDTH), jnp.bfloat16),
            pltpu.VMEM((OWNED, WIDTH), jnp.bfloat16),
            pltpu.VMEM((2, 2 * CHIPS, OWNED, WIDTH), jnp.bfloat16),
            pltpu.VMEM((BLOCK, OWNED), jnp.bfloat16),
            pltpu.VMEM((BLOCK, OWNED), jnp.bfloat16),
            pltpu.VMEM((CHIPS, 2, WIDTH, OWNED), jnp.float32),
            pltpu.VMEM((2, CHIPS, WIDTH, OWNED), jnp.float32),
            pltpu.VMEM((CHIPS, WIDTH, OWNED), jnp.int16),
            pltpu.VMEM((CHIPS, 8, OWNED), jnp.float32),
            pltpu.VMEM((2, CHIPS, WIDTH, OWNED), jnp.int16),
            pltpu.VMEM((2, CHIPS, 8, OWNED), jnp.float32),
            pltpu.VMEM((WIDTH, OWNED), jnp.float32),
            dma((6,)),
            dma((2, 2 * CHIPS)),
            dma((2, 2 * CHIPS)),
            dma((2, CHIPS)),
            dma((2, CHIPS)),
            dma((2, CHIPS)),
            dma((2, CHIPS)),
            dma((2, CHIPS)),
            dma((2, CHIPS)),
            dma((4,)),
            dma((4,)),
        ],
        compiler_params=pltpu.CompilerParams(
            collective_id=0, has_side_effects=True, vmem_limit_bytes=60 * 1024 * 1024
        ),
    )(slots, u_factors, v_factors, ratings[0, 0], u_noise, v_noise)


def solution(mesh):
    placed = (
        P(("user", "item"), None),
        P(("item", "user"), None),
        P("user", "item", None, None, None, None),
        P("user", "item", None, None),
        P("user", "item", None, None),
        P("user", "item", None),
        P(None, ("user", "item"), None),
        P(None, ("item", "user"), None),
    )
    return jax.shard_map(
        body,
        mesh=mesh,
        in_specs=placed,
        out_specs=(P(("user", "item"), None), P(("item", "user"), None)),
        check_vma=False,
    )
```

```python
import math

import jax
import jax.numpy as jnp
from jax import lax
from jax.experimental import pallas as pl
from jax.experimental.pallas import tpu as pltpu
from jax.sharding import PartitionSpec as P

HALF_STEP = 0.002
ROOT_STEP = math.sqrt(0.004)
PRIOR = 25.0
LEVELS = 32767.0
MESH = pl.DeviceIdType.MESH

TILE = 128
WIDTH = 256
BLOCK = 2048
OWNED = 256
CHIPS = 8
ITEM_PEERS = 8
BAND = 256
BANDS = BLOCK // BAND


VISIT_Y = (0, 0, 1, 0, 1, 1, 1, 0)
VISIT_X = (0, 1, 0, 2, 1, 2, 3, 3)
SWAP = 6


def pick(o, table):
    total = 0
    for k, value in enumerate(table):
        if value:
            total = total + jnp.where(o == k, value, 0)
    return total


def offset(chip, dy, dx):
    return lax.rem(chip // 4 + dy, 2) * 4 + lax.rem(lax.rem(chip, 4) + 4 + dx, 4)


def visit(o, chip):
    return offset(chip, pick(o, VISIT_Y), pick(o, VISIT_X))


def visitor(o, chip):
    return offset(chip, pick(o, VISIT_Y), -pick(o, VISIT_X))


def whole_kernel(
    power,
    slots,
    u_hbm,
    v_hbm,
    rating_hbm,
    un_hbm,
    vn_hbm,
    uout_hbm,
    vout_hbm,
    ratings_0,
    ratings_1,
    u_now,
    u_bf,
    u_turned,
    grad_u,
    u_noise,
    v_now,
    v_noise,
    noise_home,
    v_bf,
    group,
    misfit_a,
    misfit_b,
    grad_v,
    from_twin,
    packed,
    scales,
    packed_in,
    scales_in,
    total,
    load_sem,
    ag_send,
    ag_recv,
    twin_send,
    twin_recv,
    q_send,
    q_recv,
    s_send,
    s_recv,
    hop_send,
    hop_recv,
):
    user = lax.axis_index("user")
    item = lax.axis_index("item")
    chip = user // 2
    core = lax.rem(user, 2)
    twin = (chip * 2 + 1 - core, item)
    across = offset(chip, 1, 0) * 2 + core
    next_item = lax.rem(item + 1, ITEM_PEERS)
    last_item = lax.rem(item + ITEM_PEERS - 1, ITEM_PEERS)
    onward = (across, next_item)
    back = (across, last_item)

    def seen(o):
        return (visit(o, chip) * 2 + core, item)

    def at(dy, dx):
        return (offset(chip, dy, dx) * 2 + core, item)

    ratings = (ratings_0, ratings_1)
    load_v = pltpu.make_async_copy(v_hbm, v_now, load_sem.at[0])
    load_u = pltpu.make_async_copy(u_hbm, u_now, load_sem.at[1])
    load_0 = pltpu.make_async_copy(rating_hbm.at[0], ratings_0, load_sem.at[2])
    load_un = pltpu.make_async_copy(un_hbm, u_noise, load_sem.at[3])
    load_vn = pltpu.make_async_copy(vn_hbm, v_noise, load_sem.at[4])
    load_1 = pltpu.make_async_copy(rating_hbm.at[1], ratings_1, load_sem.at[5])
    barrier = pltpu.get_barrier_semaphore()
    for peer in [onward, back, (user, next_item), (user, last_item), twin]:
        pl.semaphore_signal(barrier, inc=1, device_id=peer, device_id_type=MESH)

    def greet(o, _):
        pl.semaphore_signal(barrier, inc=1, device_id=seen(CHIPS - o), device_id_type=MESH)
        return 0

    lax.fori_loop(1, CHIPS, greet, 0)
    load_v.start()
    load_u.start()
    load_0.start()
    load_vn.start()

    def remote(src, dst, send, recv, device):
        return pltpu.make_async_remote_copy(
            src_ref=src, dst_ref=dst, send_sem=send, recv_sem=recv, device_id=device, device_id_type=MESH
        )

    noise_copy = remote(v_noise.at[1], noise_home, hop_send.at[1], hop_recv.at[1], (user, last_item))

    def ag_copy(s, owner, lane, device):
        at = group.at[s, owner]
        return remote(at, at, ag_send.at[s, lane], ag_recv.at[s, owner], device)

    def spread(s):
        ag_copy(s, user, 0, twin).start()
        ag_copy(s, user, 1, at(0, 1)).start()
        ag_copy(s, user, 2, at(0, -1)).start()
        ag_copy(s, user, 3, at(1, 0)).start()

    def pass_on(s, order, dy, dx):
        owner = offset(chip, dy, dx) * 2 + core
        ag_copy(s, owner, 0, twin).wait_recv()
        ag_copy(s, owner, CHIPS + order, twin).start()
        if (dy, dx) == (1, 0):
            ag_copy(s, owner, 5, at(0, 1)).start()
            ag_copy(s, owner, 6, at(0, -1)).start()
        if (dy, dx) == (0, 2):
            ag_copy(s, owner, 7, at(1, 0)).start()
        if (dy, dx) == (0, -1):

            @pl.when(core == 0)
            def _():
                ag_copy(s, owner, 4, at(0, 1)).start()

        if (dy, dx) == (0, 1):

            @pl.when(core == 1)
            def _():
                ag_copy(s, owner, 4, at(0, -1)).start()

    def twin_copy(s, o):
        return remote(
            grad_v.at[o, 1 - core], from_twin.at[s, o], twin_send.at[s, o], twin_recv.at[s, o], twin
        )

    def q_copy(s, o, slot):
        return remote(packed.at[o], packed_in.at[s, slot], q_send.at[s, o], q_recv.at[s, slot], seen(o))

    def s_copy(s, o, slot):
        return remote(scales.at[o], scales_in.at[s, slot], s_send.at[s, o], s_recv.at[s, slot], seen(o))

    def prepare(s):
        def one(b, _):
            rows = pl.ds(pl.multiple_of(b * BAND, BAND), BAND)
            now = u_now[rows, :]
            if s > 0:
                now = (
                    now
                    + HALF_STEP * (power * grad_u[rows, :] - PRIOR * now)
                    + ROOT_STEP * u_noise[s - 1, rows, :].astype(jnp.float32)
                )
                u_now[rows, :] = now
            if s < 2:
                u_bf[rows, :] = now.astype(jnp.bfloat16)
                u_turned[:, rows] = now.T.astype(jnp.bfloat16)
                grad_u[rows, :] = jnp.zeros((BAND, WIDTH), jnp.float32)
            return 0

        lax.fori_loop(0, BANDS, one, 0)

    def predict(s, owner, misfit):
        items = group[s, owner]
        tiles = 2 * (owner if s == 0 else lax.rem(owner + 8, 16))
        for b in range(BANDS):
            rows = pl.ds(b * BAND, BAND)
            predicted = lax.dot_general(
                u_bf[rows, :], items, (((1,), (1,)), ((), ())), preferred_element_type=jnp.float32
            )
            for i in range(BAND // TILE):
                for j in range(OWNED // TILE):
                    at = slots[s, (b * (BAND // TILE) + i) * 32 + tiles + j]
                    rating = ratings[s][jnp.maximum(at, 0)].astype(jnp.float32)
                    part = predicted[i * TILE : (i + 1) * TILE, j * TILE : (j + 1) * TILE]
                    misfit[pl.ds(b * BAND + i * TILE, TILE), pl.ds(j * TILE, TILE)] = jnp.where(
                        at >= 0, rating - part, 0.0
                    ).astype(jnp.bfloat16)

    def grads(s, o, owner, half, misfit):
        items = group[s, owner]
        for b in range(BANDS):
            rows = pl.ds(b * BAND, BAND)
            grad_u[rows, :] += jnp.dot(misfit[rows, :], items, preferred_element_type=jnp.float32)
        grad_v[o, half] = jnp.dot(u_turned[...], misfit[...], preferred_element_type=jnp.float32)

    def coded(term):
        peak = jnp.max(jnp.abs(term), axis=0, keepdims=True)
        inverse = jnp.where(peak > 1e-30, LEVELS / jnp.maximum(peak, 1e-30), 0.0)
        code = jnp.round(term * inverse).astype(jnp.int32).astype(jnp.int16)
        return code, jnp.broadcast_to(peak * (1.0 / LEVELS), (8, OWNED))

    def decoded(code, step):
        return code.astype(jnp.int32).astype(jnp.float32) * step[0:1, :]

    def finish(s, o):
        twin_copy(s, o).wait_recv()
        packed[o], scales[o] = coded(grad_v[o, core] + from_twin[s, o])
        q_copy(s, o, chip).start()
        s_copy(s, o, chip).start()

    def half_of(o, second):
        first = jnp.where(o < SWAP, core, 1 - core)
        return 1 - first if second else first

    def owner_of(o, second):
        return visit(o, chip) * 2 + half_of(o, second)

    def await_twin(s, o):
        ag_copy(s, visit(o, chip) * 2 + 1 - core, 0, twin).wait_recv()

    def first_block(s, o):
        @pl.when(o < SWAP)
        def _():
            await_twin(s, o)

        predict(s, owner_of(o, True), misfit_b)
        grads(s, o, owner_of(o, False), half_of(o, False), misfit_a)

        @pl.when(o >= SWAP)
        def _():
            twin_copy(s, o).start()

        @pl.when(o > 1)
        def _():
            finish(s, o - 1)

    def section(s):
        predict(s, user, misfit_a)

        def meet(o, _):
            first_block(s, o)

            @pl.when(o == 0)
            def _():
                pass_on(s, 3, 0, 1)

            @pl.when(o == 2)
            def _():
                pass_on(s, 6, 0, 2)

            @pl.when(o == 4)
            def _():
                pass_on(s, 7, 1, 2)

            @pl.when(o + 1 >= SWAP)
            def _():
                await_twin(s, o + 1)

            predict(s, owner_of(o + 1, False), misfit_a)
            grads(s, o, owner_of(o, True), half_of(o, True), misfit_b)

            @pl.when(o < SWAP)
            def _():
                twin_copy(s, o).start()

            @pl.when(o == 0)
            def _():
                pass_on(s, 2, 1, 0)
                pass_on(s, 1, 0, -1)

            @pl.when(o == 2)
            def _():
                pass_on(s, 5, 1, 1)
                pass_on(s, 4, 1, -1)

            if s == 0:

                @pl.when(o == 1)
                def _():
                    load_1.start()
                    load_un.start()

                @pl.when(o == 5)
                def _():
                    noise_copy.start()

            return 0

        lax.fori_loop(0, CHIPS - 1, meet, 0)
        last = CHIPS - 1
        first_block(s, last)
        grads(s, last, owner_of(last, True), half_of(last, True), misfit_b)
        finish(s, last)

    def own_sum(s):
        twin_copy(s, 0).wait_recv()
        total[...] = grad_v[0, core] + from_twin[s, 0]

        def add(o, _):
            slot = visitor(o, chip)
            q_copy(s, o, slot).wait_recv()
            s_copy(s, o, slot).wait_recv()
            total[...] += decoded(packed_in[s, slot], scales_in[s, slot])
            return 0

        lax.fori_loop(1, CHIPS, add, 0)

    def settle(s):
        ag_copy(s, user, 0, twin).wait_send()
        twin_copy(s, 0).wait_send()

        def one(o, _):
            ag_copy(s, user, o, twin).wait_send()
            ag_copy(s, user, CHIPS + o, twin).wait_send()
            twin_copy(s, o).wait_send()
            q_copy(s, o, chip).wait_send()
            s_copy(s, o, chip).wait_send()
            return 0

        lax.fori_loop(1, CHIPS, one, 0)

    load_u.wait()
    prepare(0)
    load_v.wait()
    group[0, user] = v_now[...].astype(jnp.bfloat16)
    load_vn.wait()
    load_0.wait()
    pl.semaphore_wait(barrier, 5 + CHIPS - 1)
    spread(0)
    section(0)
    load_un.wait()
    prepare(1)
    own_sum(0)
    now = v_now[...]
    now = now + HALF_STEP * (power * total[...].T - PRIOR * now) + ROOT_STEP * v_noise[0].astype(jnp.float32)
    v_bf[...] = now.astype(jnp.bfloat16)
    hop = remote(v_bf, group.at[1, across], hop_send.at[0], hop_recv.at[0], onward)
    hop.start()
    v_now[...] = now
    settle(0)
    hop.wait_recv()

    spread(1)
    load_1.wait()
    section(1)
    prepare(2)
    store_u = pltpu.make_async_copy(u_now, uout_hbm, load_sem.at[1])
    store_u.start()
    own_sum(1)
    packed[0], scales[0] = coded(total[...])
    home = offset(chip, 1, 0)
    home_q = remote(packed.at[0], packed_in.at[1, home], hop_send.at[2], hop_recv.at[2], back)
    home_s = remote(scales.at[0], scales_in.at[1, home], hop_send.at[3], hop_recv.at[3], back)
    home_q.start()
    home_s.start()
    settle(1)
    hop.wait_send()
    noise_copy.wait()
    now = v_now[...]
    now = now - HALF_STEP * PRIOR * now + ROOT_STEP * noise_home[...].astype(jnp.float32)
    home_q.wait()
    home_s.wait()
    v_now[...] = now + HALF_STEP * power * decoded(packed_in[1, chip], scales_in[1, chip]).T
    store_v = pltpu.make_async_copy(v_now, vout_hbm, load_sem.at[0])
    store_v.start()
    store_u.wait()
    store_v.wait()


def slot_map(rows, cols, counts):
    slot = jnp.arange(rows.shape[1], dtype=jnp.int32)
    cell = jnp.arange(512, dtype=jnp.int32)
    held = jnp.where(slot < counts[:, None], rows * 32 + cols, -1)
    return jnp.max(jnp.where(held[:, None, :] == cell[None, :, None], slot, -1), axis=2)


def body(u_factors, v_factors, ratings, tile_rows, tile_cols, tile_counts, u_noise, v_noise):
    slots = slot_map(tile_rows[0, 0], tile_cols[0, 0], tile_counts[0, 0])
    listed = ratings.shape[3]
    power = float(lax.axis_size("item"))
    anywhere = pl.BlockSpec(memory_space=pl.ANY)
    dma = pltpu.SemaphoreType.DMA

    def kernel(*refs):
        whole_kernel(power, *refs)

    return pl.pallas_call(
        kernel,
        out_shape=(
            jax.ShapeDtypeStruct(u_factors.shape, jnp.float32),
            jax.ShapeDtypeStruct(v_factors.shape, jnp.float32),
        ),
        in_specs=[pl.BlockSpec(memory_space=pltpu.SMEM)] + [anywhere] * 5,
        out_specs=(anywhere, anywhere),
        scratch_shapes=[
            pltpu.VMEM((listed, TILE, TILE), jnp.bfloat16),
            pltpu.VMEM((listed, TILE, TILE), jnp.bfloat16),
            pltpu.VMEM((BLOCK, WIDTH), jnp.float32),
            pltpu.VMEM((BLOCK, WIDTH), jnp.bfloat16),
            pltpu.VMEM((WIDTH, BLOCK), jnp.bfloat16),
            pltpu.VMEM((BLOCK, WIDTH), jnp.float32),
            pltpu.VMEM((2, BLOCK, WIDTH), jnp.bfloat16),
            pltpu.VMEM((OWNED, WIDTH), jnp.float32),
            pltpu.VMEM((2, OWNED, WIDTH), jnp.bfloat16),
            pltpu.VMEM((OWNED, WIDTH), jnp.bfloat16),
            pltpu.VMEM((OWNED, WIDTH), jnp.bfloat16),
            pltpu.VMEM((2, 2 * CHIPS, OWNED, WIDTH), jnp.bfloat16),
            pltpu.VMEM((BLOCK, OWNED), jnp.bfloat16),
            pltpu.VMEM((BLOCK, OWNED), jnp.bfloat16),
            pltpu.VMEM((CHIPS, 2, WIDTH, OWNED), jnp.float32),
            pltpu.VMEM((2, CHIPS, WIDTH, OWNED), jnp.float32),
            pltpu.VMEM((CHIPS, WIDTH, OWNED), jnp.int16),
            pltpu.VMEM((CHIPS, 8, OWNED), jnp.float32),
            pltpu.VMEM((2, CHIPS, WIDTH, OWNED), jnp.int16),
            pltpu.VMEM((2, CHIPS, 8, OWNED), jnp.float32),
            pltpu.VMEM((WIDTH, OWNED), jnp.float32),
            dma((6,)),
            dma((2, 2 * CHIPS)),
            dma((2, 2 * CHIPS)),
            dma((2, CHIPS)),
            dma((2, CHIPS)),
            dma((2, CHIPS)),
            dma((2, CHIPS)),
            dma((2, CHIPS)),
            dma((2, CHIPS)),
            dma((4,)),
            dma((4,)),
        ],
        compiler_params=pltpu.CompilerParams(
            collective_id=0, has_side_effects=True, vmem_limit_bytes=60 * 1024 * 1024
        ),
    )(slots, u_factors, v_factors, ratings[0, 0], u_noise, v_noise)


def solution(mesh):
    placed = (
        P(("user", "item"), None),
        P(("item", "user"), None),
        P("user", "item", None, None, None, None),
        P("user", "item", None, None),
        P("user", "item", None, None),
        P("user", "item", None),
        P(None, ("user", "item"), None),
        P(None, ("item", "user"), None),
    )
    return jax.shard_map(
        body,
        mesh=mesh,
        in_specs=placed,
        out_specs=(P(("user", "item"), None), P(("item", "user"), None)),
        check_vma=False,
    )
```
